512 devices in a mesh: req: 32 (over z, x), head: 16 (over y, core).
Axes of the slice: x: 4, y: 8, z: 8, core: 2. Of those that a mesh axis runs over, the one named last changes fastest.
Arguments:
- suffix_embeddings: bfloat16 [1024, 16, 4096], P('req', None, 'head'), may hold values from -6 to 6
- suffix_extents: int32 [1024], replicated, may hold values from 4 to 16, as said below
- memory_line_pointer: int32 [1024], replicated, may hold values from 0 to 1023, as said below
- previous_token_store: bfloat16 [1024, 4096], P('req', 'head'), may hold values from -6 to 6
- stored_memories: bfloat16 [1024, 64, 4096], P('req', 'head'), may hold values from -4 to 4
- blend_fractions: float32 [4, 4096], replicated, may hold values from 0 to 1
- acceptor_linear: bfloat16 [4096, 4096], P('req', 'head'), may hold values from -0.09375 to 0.09375
- address_linear: bfloat16 [4096, 4096], P('req', 'head'), may hold values from -0.09375 to 0.09375
- payload_linear: bfloat16 [4096, 4096], P('req', 'head'), may hold values from -0.09375 to 0.09375
- fading_baseline: float32 [4096], P('head'), may hold values from -5 to 0
- fading_bottleneck_down: bfloat16 [4096, 128], replicated, may hold values from -0.09375 to 0.09375
- fading_bottleneck_up: bfloat16 [128, 4096], P(None, 'head'), may hold values from -0.5 to 0.5
- self_reward: float32 [4096], P('head'), may hold values from -3 to 3
- team_normalizer_gain: float32 [4096], P('head'), may hold values from 0.5 to 1.5
Outputs:
- mixed_out: bfloat16 [1024, 16, 4096], P('req', None, 'head')
- new_state: bfloat16 [1024, 64, 4096], P('req', 'head')
- new_shift: bfloat16 [1024, 4096], P('req', 'head')
The draws below stay inside these ranges and needn't reach their ends.
Inputs may be any that keep to these rules, and one draw needn't show every extreme that they name: `suffix_extents`: some request has exactly 16 live tokens and some has 4. `memory_line_pointer`: A permutation of the cache rows; rows r with equal r // 32 form one owner. For each serving group (the 32 requests s with equal s // 32) and each owner, either exactly 2 or none of the group's requests have their row at that owner.
All inputs are finite; a program needn't handle non-finite values.
Results may differ from the reference program's by a relative error of at most 0.0083.
Values may be sent and summed in bfloat16 or wider, within the bound.
A program may use at most 128 MiB of HBM per device.

```python
import jax
import jax.numpy as jnp
from jax import lax

EMBEDDING_DIM = 4096
ATTENTION_TEAMS = 64
DR = 128
R_DEV = 32
LMAX = 16
TEAM_BREADTH = 64
REQS = 1024
MOST = 2
PEERS = 16


def order_of(sub_key):
    return jax.random.permutation(sub_key, R_DEV)


def draw_memory_line_pointer(key, part):
    groups = REQS // R_DEV
    base = jax.random.fold_in(key, 17)
    shift_key, owner_key, order_key = jax.random.split(base, 3)
    offsets = jax.random.permutation(shift_key, groups)[:PEERS]
    group_ids = jnp.arange(groups, dtype=jnp.int32)[:, None, None]
    block_ids = jnp.arange(PEERS, dtype=jnp.int32)[None, :, None]
    slot_ids = jnp.arange(MOST, dtype=jnp.int32)[None, None, :]
    owners = jnp.broadcast_to((group_ids + offsets[None, :, None]) % groups, (groups, PEERS, MOST))
    inner = jnp.broadcast_to(block_ids * MOST + slot_ids, (groups, PEERS, MOST))
    owner_orders = jax.vmap(order_of)(jax.random.split(owner_key, groups))
    within = owner_orders[owners, inner]
    cache_rows = (owners * R_DEV + within).reshape(groups, R_DEV)
    group_orders = jax.vmap(order_of)(jax.random.split(order_key, groups))
    placed = jnp.take_along_axis(cache_rows, group_orders, axis=1)
    return placed.reshape(-1).astype(jnp.int32)


def draw_suffix_extents(key, part):
    groups = REQS // R_DEV
    base = jax.random.fold_in(key, 29)
    pick_key, long_key, short_key = jax.random.split(base, 3)
    heavy_count = max(1, groups // 8)
    heavy = jax.random.permutation(pick_key, groups)[:heavy_count]
    is_heavy = jnp.any(jnp.arange(groups, dtype=jnp.int32)[:, None] == heavy[None, :], axis=1)
    long_draw = jax.random.randint(long_key, (groups, R_DEV), LMAX - LMAX // 4, LMAX + 1)
    short_draw = jax.random.randint(short_key, (groups, R_DEV), LMAX // 4, LMAX // 2 + 1)
    chosen = jnp.where(is_heavy[:, None], long_draw, short_draw)
    chosen = chosen.at[heavy[0], 0].set(LMAX)
    lightest = jnp.argmin(is_heavy.astype(jnp.int32))
    chosen = chosen.at[lightest, 0].set(LMAX // 4)
    return chosen.reshape(-1).astype(jnp.int32)


def steps_of(rng, shape, cuts, least, top_value):
    loudness = 1.0
    for position, blocks in cuts:
        steps = jax.random.uniform(jax.random.fold_in(jax.random.fold_in(rng, 6), position), (blocks,), jnp.float32, least / len(cuts), top_value / len(cuts))
        loudness = loudness * jnp.repeat(jnp.exp(steps), shape[position] // blocks).reshape((-1,) + (1,) * (len(shape) - 1 - position))
    return loudness


def bell_draw(stream_key, dims, scale, most, cuts=(), held_as=jnp.bfloat16):
    entries = jax.random.normal(stream_key, dims, jnp.float32) * scale
    if len(cuts) > 0:
        entries = steps_of(stream_key, dims, cuts, -0.22, 0.18) * entries
    return jnp.clip(entries, min=-most, max=most).astype(held_as)


def setup_inputs(seed: int = 0) -> dict:
    arg_keys = jax.random.split(jax.random.key(seed), 15)
    suffix_embeddings = bell_draw(arg_keys[0], (REQS, LMAX, EMBEDDING_DIM), 1.0, 6.0, ((0, 32), (2, 16)))
    suffix_extents = draw_suffix_extents(jax.random.fold_in(arg_keys[14], 71), 0)
    memory_line_pointer = draw_memory_line_pointer(jax.random.fold_in(arg_keys[14], 71), 0)
    previous_token_store = bell_draw(arg_keys[3], (REQS, EMBEDDING_DIM), 1.0, 6.0, ((0, 32), (1, 16)))
    stored_memories = bell_draw(arg_keys[4], (REQS, ATTENTION_TEAMS, TEAM_BREADTH * TEAM_BREADTH), 0.5, 4.0, ((0, 32), (1, 16)))
    blend_fractions = jnp.clip(jax.random.uniform(arg_keys[5], (4, EMBEDDING_DIM), jnp.float32, 0.0, 1.0), 0.0, 1.0)
    acceptor_linear = bell_draw(arg_keys[6], (EMBEDDING_DIM, EMBEDDING_DIM), EMBEDDING_DIM ** -0.5, 0.09375, ((0, 32), (1, 16)))
    address_linear = bell_draw(arg_keys[7], (EMBEDDING_DIM, EMBEDDING_DIM), EMBEDDING_DIM ** -0.5, 0.09375, ((0, 32), (1, 16)))
    payload_linear = bell_draw(arg_keys[8], (EMBEDDING_DIM, EMBEDDING_DIM), EMBEDDING_DIM ** -0.5, 0.09375, ((0, 32), (1, 16)))
    fading_baseline = jnp.clip(-5.0 + 5.0 * jax.random.uniform(arg_keys[9], (EMBEDDING_DIM,), jnp.float32) ** steps_of(arg_keys[9], (EMBEDDING_DIM,), ((0, 16),), -0.2, 0.2), -5.0, 0.0)
    fading_bottleneck_down = bell_draw(arg_keys[10], (EMBEDDING_DIM, DR), EMBEDDING_DIM ** -0.5, 0.09375)
    fading_bottleneck_up = bell_draw(arg_keys[11], (DR, EMBEDDING_DIM), DR ** -0.5, 0.5, ((1, 16),))
    self_reward = bell_draw(arg_keys[12], (EMBEDDING_DIM,), 0.5, 3.0, ((0, 16),), jnp.float32)
    team_normalizer_gain = jnp.clip(1.0 + 0.1 * jax.random.normal(arg_keys[13], (EMBEDDING_DIM,), jnp.float32), 0.5, 1.5)
    return dict(suffix_embeddings=suffix_embeddings, suffix_extents=suffix_extents, memory_line_pointer=memory_line_pointer, previous_token_store=previous_token_store, stored_memories=stored_memories, blend_fractions=blend_fractions, acceptor_linear=acceptor_linear, address_linear=address_linear, payload_linear=payload_linear, fading_baseline=fading_baseline, fading_bottleneck_down=fading_bottleneck_down, fading_bottleneck_up=fading_bottleneck_up, self_reward=self_reward, team_normalizer_gain=team_normalizer_gain)


EPS = 0.00064

def mixed_input(current, earlier, coefficient):
    return (current + (earlier - current) * coefficient).astype(jnp.bfloat16).reshape(REQS * LMAX, EMBEDDING_DIM)

def team_refresh(sweep_arguments):
    acceptor_entries, address_entries, payload_array, fading_exponent, leading_reward_team, starting_memory = sweep_arguments

    def advance(evolving_memory, inputs):
        present_acceptor, present_address, present_payload, decay_now = inputs
        produced_outputs = jnp.einsum('ni,nij->nj', present_acceptor, evolving_memory, precision=lax.Precision.HIGHEST)
        produced_outputs = produced_outputs + lax.optimization_barrier(jnp.sum(present_acceptor * leading_reward_team * present_address, axis=-1, keepdims=True)) * present_payload
        evolving_memory = jnp.exp(decay_now)[:, :, None] * evolving_memory + present_address[:, :, None] * present_payload[:, None, :]
        return (evolving_memory, produced_outputs)
    final_memory, emitted_all = lax.scan(advance, starting_memory, (acceptor_entries, address_entries, payload_array, fading_exponent))
    return (emitted_all, final_memory)

def team_ordered_entries(array_in):
    return jnp.transpose(array_in.astype(jnp.float32).reshape(REQS, LMAX, ATTENTION_TEAMS, TEAM_BREADTH), (2, 1, 0, 3))

def reference(suffix_embeddings, suffix_extents, memory_line_pointer, previous_token_store, stored_memories, blend_fractions, acceptor_linear, address_linear, payload_linear, fading_baseline, fading_bottleneck_down, fading_bottleneck_up, self_reward, team_normalizer_gain):
    prior_shift = previous_token_store[memory_line_pointer]
    previous = jnp.concatenate([prior_shift[:, None, :], suffix_embeddings[:, :-1, :]], axis=1)
    alive_mask = (jnp.arange(LMAX, dtype=jnp.int32)[None, :] < suffix_extents[:, None]).reshape(REQS * LMAX, 1)
    current = suffix_embeddings.astype(jnp.float32)
    earlier = previous.astype(jnp.float32)
    acceptor_entries = jnp.dot(mixed_input(current, earlier, blend_fractions[0]), acceptor_linear, preferred_element_type=jnp.float32).astype(jnp.bfloat16)
    address_entries = jnp.dot(mixed_input(current, earlier, blend_fractions[1]), address_linear, preferred_element_type=jnp.float32).astype(jnp.bfloat16)
    payload_array = jnp.dot(mixed_input(current, earlier, blend_fractions[2]), payload_linear, preferred_element_type=jnp.float32).astype(jnp.bfloat16)
    address_entries = jnp.where(alive_mask, address_entries, jnp.zeros((), jnp.bfloat16))
    low_rank_delta = jnp.tanh(jnp.dot(mixed_input(current, earlier, blend_fractions[3]), fading_bottleneck_down, preferred_element_type=jnp.float32)).astype(jnp.bfloat16)
    fading_exponent = fading_baseline + jnp.dot(low_rank_delta, fading_bottleneck_up, preferred_element_type=jnp.float32)
    fading_exponent = jnp.where(alive_mask, -jnp.exp(fading_exponent), jnp.zeros((), jnp.float32))
    starting_memory = jnp.transpose(stored_memories[memory_line_pointer].astype(jnp.float32).reshape(REQS, ATTENTION_TEAMS, TEAM_BREADTH, TEAM_BREADTH), (1, 0, 2, 3))
    produced_outputs, final_memory = lax.map(team_refresh, (team_ordered_entries(acceptor_entries), team_ordered_entries(address_entries), team_ordered_entries(payload_array), team_ordered_entries(fading_exponent), self_reward.reshape(ATTENTION_TEAMS, TEAM_BREADTH), starting_memory))
    outputs = jnp.transpose(produced_outputs, (2, 1, 0, 3))
    center = outputs - lax.optimization_barrier(jnp.mean(outputs, axis=-1, keepdims=True))
    spread = lax.optimization_barrier(jnp.mean(center * center, axis=-1, keepdims=True))
    normed = center * lax.rsqrt(spread + EPS) * team_normalizer_gain.reshape(ATTENTION_TEAMS, TEAM_BREADTH)
    alive_four = alive_mask.reshape(REQS, LMAX, 1, 1)
    mixed_out = jnp.where(alive_four, normed, jnp.zeros((), jnp.float32)).astype(jnp.bfloat16).reshape(REQS, LMAX, EMBEDDING_DIM)
    state_rows = jnp.transpose(final_memory, (1, 0, 2, 3)).reshape(REQS, ATTENTION_TEAMS, TEAM_BREADTH * TEAM_BREADTH).astype(jnp.bfloat16)
    new_state = jnp.zeros_like(stored_memories).at[memory_line_pointer].set(state_rows)
    last_token = suffix_embeddings[jnp.arange(REQS, dtype=jnp.int32), suffix_extents - 1]
    new_shift = jnp.zeros_like(previous_token_store).at[memory_line_pointer].set(last_token)
    return (mixed_out, new_state, new_shift)
```

```python
import jax
import jax.numpy as jnp
from jax import lax
from jax.experimental import pallas as pl
from jax.experimental.pallas import tpu as pltpu
from jax.sharding import PartitionSpec as P

F32, BF16 = jnp.float32, jnp.bfloat16
HIGHEST = lax.Precision.HIGHEST
ROWS, LENGTH, WIDTH, TEAMS, TEAM_BREADTH = 32, 16, 256, 4, 64
TOKENS = ROWS * LENGTH
EPS = 0.00064


def mm(a, b):
    return lax.dot_general(a, b, (((1,), (0,)), ((), ())), preferred_element_type=F32)


def mm_nt(a, b):
    return lax.dot_general(a, b, (((1,), (1,)), ((), ())), preferred_element_type=F32)


def mm_tn(a, b, precision=None):
    return lax.dot_general(a, b, (((0,), (0,)), ((), ())), preferred_element_type=F32, precision=precision)


def take(ref, rows):
    return jnp.concatenate([ref[0, rows, :], ref[1, rows, :]], axis=1)


def put(ref, rows, value):
    ref[0, rows, :] = value[:, :128]
    ref[1, rows, :] = value[:, 128:]


def iota(shape, dim):
    return lax.broadcasted_iota(jnp.int32, shape, dim)


def recurrence_kernel(
    slot_ref, r_ref, k_ref, v_ref, low_ref, up_ref, base_ref, reward_ref, gain_ref, extent_ref, state_ref, token_ref,
    out_ref, state_out, shift_out,
    rp, kp, vf, dl, y, rin, kout, decay_all,
):
    a = iota((WIDTH, WIDTH), 0)
    target = (a & 1) * 128 + ((a >> 1) & 31) * 4 + (a >> 6)
    moved = iota((WIDTH, WIDTH), 1) == target
    perm = jnp.where(moved, 1.0, 0.0).astype(BF16)
    perm_f = jnp.where(moved, 1.0, 0.0)
    rp[...] = mm(r_ref[...], perm)
    kp[...] = mm(k_ref[...], perm)
    put(vf, slice(None), v_ref[...].astype(F32))
    row8 = iota((8, WIDTH), 0)
    both = jnp.where(row8 == 0, base_ref[...], jnp.where(row8 == 1, reward_ref[...], 0.0))
    both = lax.dot_general(both, perm_f, (((1,), (0,)), ((), ())), preferred_element_type=F32, precision=HIGHEST)
    base, reward = both[0:1], both[1:2]
    dl[...] = mm(low_ref[...], mm(up_ref[...], perm).astype(BF16)) + base
    out_ref[...] = jnp.zeros_like(out_ref)

    extent = jnp.broadcast_to(extent_ref[:, 0:1], (ROWS, WIDTH))
    last = jnp.zeros((ROWS, WIDTH), F32)
    for t in range(LENGTH):
        last = jnp.where(extent == t + 1, token_ref[t * ROWS : (t + 1) * ROWS].astype(F32), last)
    shift_out[...] = last.astype(BF16)

    lane = iota((1, WIDTH), 1)
    ri, ci = iota((128, 128), 0), iota((128, 128), 1)
    same = (ri & 7) == (ci & 7)
    rt, ct = ri >> 3, ci >> 3

    @pl.loop(0, ROWS // 8)
    def group(g):
        at = pl.multiple_of(g * 8, 8)

        def rows_of(ref):
            return [ref[pl.ds(pl.multiple_of(t * ROWS + at, 8), 8), :] for t in range(LENGTH)]

        ext = jnp.broadcast_to(extent_ref[pl.ds(at, 8), 0:1], (8, WIDTH))
        d = [jnp.where(ext > t, -jnp.exp(x), 0.0) for t, x in enumerate(rows_of(dl))]
        r = rows_of(rp)
        k = [jnp.where(ext > t, x, 0.0) for t, x in enumerate(rows_of(kp))]
        vals = [take(vf, pl.ds(pl.multiple_of(t * ROWS + at, 8), 8)) for t in range(LENGTH)]
        vals = jnp.concatenate(vals, axis=0).astype(BF16)
        totals, before, after = list(d), [None] * LENGTH, [None] * LENGTH

        def scaled(x, e):
            return x if e is None else x * jnp.exp(e)

        def stack(xs):
            return jnp.concatenate(xs, axis=0).astype(BF16)

        def scores(left, right, keep, so_far):
            right = stack(right)
            left = stack(left)
            res = []
            for h in range(TEAMS):
                s = mm_nt(jnp.where((lane & 3) == h, left, jnp.zeros((), BF16)), right)
                s = jnp.where(keep, s, 0.0)
                res.append(s if so_far is None else so_far[h] + s)
            return res

        total = scores([x * reward for x in r], k, same & (rt == ct), None)
        size = 1
        while size < LENGTH:
            late = [scaled(r[t], before[t]) if (t // size) & 1 else r[t] for t in range(LENGTH)]
            early = [k[t] if (t // size) & 1 else scaled(k[t], after[t]) for t in range(LENGTH)]
            sh = size.bit_length()
            keep = same & ((rt >> sh) == (ct >> sh)) & ((rt & size) != 0) & ((ct & size) == 0)
            total = scores(late, early, keep, total)
            for t in range(LENGTH):
                b = t // size
                if b & 1:
                    before[t] = totals[b - 1] if before[t] is None else before[t] + totals[b - 1]
                else:
                    after[t] = totals[b + 1] if after[t] is None else after[t] + totals[b + 1]
            totals = [totals[2 * b] + totals[2 * b + 1] for b in range(len(totals) // 2)]
            size *= 2
        mixed = None
        for h in range(TEAMS):
            part = mm(total[h].astype(BF16), jnp.where((lane >> 6) == h, vals, jnp.zeros((), BF16)))
            mixed = part if mixed is None else mixed + part
        for t in range(LENGTH):
            where = pl.ds(pl.multiple_of(t * ROWS + at, 8), 8)
            put(y, where, mixed[t * 8 : (t + 1) * 8])
            put(rin, where, scaled(r[t], before[t]))
            put(kout, where, scaled(k[t], after[t]))
        put(decay_all, pl.ds(at, 8), jnp.exp(totals[0]))

    lane128 = iota((LENGTH, 128), 1)
    low_half = lane128 < 64
    row_8, lane_8 = iota((8, 128), 0), iota((8, 128), 1)
    picks = jnp.where(((row_8 == 0) & (lane_8 < 64)) | ((row_8 == 1) & (lane_8 >= 64)), 1.0, 0.0)

    def spread(x):
        pieces = []
        for p in range(2):
            piece = x[p]
            for h in range(TEAMS):
                pieces.append(jnp.where((lane128 & 3) == h, piece, 0.0))
        return jnp.concatenate(pieces, axis=0).astype(BF16)

    def one_row(n, carry):
        where = pl.ds(n, LENGTH, stride=ROWS)
        state = state_ref[n]
        halves = []
        o = mm(spread([rin[p, where, :] for p in range(2)]), state)
        part = lambda p, h: o[(p * 4 + h) * 16 : (p * 4 + h + 1) * 16]
        for e in range(2):
            direct = jnp.where(low_half, part(0, 2 * e), part(1, 2 * e + 1))
            crossed = jnp.where(low_half, part(0, 2 * e + 1), part(1, 2 * e))
            halves.append(direct + pltpu.roll(crossed, 64, 1))
        for e in range(2):
            y[e, where, :] = y[e, where, :] + halves[e]
        keys = spread([kout[p, where, :] for p in range(2)])
        pieces = [None] * 8
        for e in range(2):
            v = vf[e, where, :]
            vr = pltpu.roll(v, 64, 1)
            pieces[2 * e] = jnp.where(low_half, v, 0.0)
            pieces[2 * e + 1] = jnp.where(low_half, vr, 0.0)
            pieces[4 + 2 * e] = jnp.where(low_half, 0.0, vr)
            pieces[4 + 2 * e + 1] = jnp.where(low_half, 0.0, v)
        update = mm_tn(keys, jnp.concatenate(pieces, axis=0).astype(BF16))
        e0, e1 = decay_all[0, pl.ds(n, 1), :], decay_all[1, pl.ds(n, 1), :]
        kept = mm_tn(jnp.where(row_8 == 0, e0, jnp.where(row_8 == 1, e1, 0.0)), picks, HIGHEST)
        state_out[n] = (kept * state.astype(F32) + update).astype(BF16)
        return carry

    lax.fori_loop(0, ROWS, one_row, 0, unroll=2)

    ones = jnp.where((iota((WIDTH, WIDTH), 0) >> 6) == (iota((WIDTH, WIDTH), 1) >> 6), 1.0 / TEAM_BREADTH, 0.0).astype(BF16)

    @pl.loop(0, 4)
    def norm(b):
        where = pl.ds(pl.multiple_of(b * 128, 128), 128)
        x = take(y, where)
        hi = x.astype(BF16)
        mean = mm(hi, ones) + mm((x - hi.astype(F32)).astype(BF16), ones)
        center = x - mean
        sq = center * center
        shi = sq.astype(BF16)
        var = mm(shi, ones) + mm((sq - shi.astype(F32)).astype(BF16), ones)
        normed = center * lax.rsqrt(var + EPS) * gain_ref[...]
        for j in range(4):
            alive = jnp.where(extent > b * 4 + j, normed[j * 32 : (j + 1) * 32], 0.0)
            put(y, pl.ds(pl.multiple_of(b * 128 + j * 32, 32), 32), alive)

    def place(n, carry):
        where = pl.ds(n, LENGTH, stride=ROWS)
        for e in range(2):
            out_ref[slot_ref[n], :, e * 128 : (e + 1) * 128] = y[e, where, :].astype(BF16)
        return carry

    lax.fori_loop(0, ROWS, place, 0, unroll=4)


def recurrence(slots, r, k, v, low, up, base, reward, gain, extents, state, tokens, interpret=False):
    vm = pl.BlockSpec(memory_space=pltpu.VMEM)
    big, split = pltpu.VMEM((TOKENS, WIDTH), F32), pltpu.VMEM((2, TOKENS, 128), F32)
    return pl.pallas_call(
        recurrence_kernel,
        out_shape=(
            jax.ShapeDtypeStruct((2 * ROWS, LENGTH, WIDTH), BF16),
            jax.ShapeDtypeStruct((ROWS, 128, 128), BF16),
            jax.ShapeDtypeStruct((ROWS, WIDTH), BF16),
        ),
        in_specs=[pl.BlockSpec(memory_space=pltpu.SMEM)] + [vm] * 11,
        out_specs=(vm, vm, vm),
        scratch_shapes=[big, big, split, big, split, split, split] + [pltpu.VMEM((2, ROWS, 128), F32)],
        name="recurrence",
        interpret=interpret,
    )(slots, r, k, v, low, up, base.reshape(1, WIDTH), reward.reshape(1, WIDTH), gain.reshape(1, WIDTH), extents, state, tokens)

MESH = pl.DeviceIdType.MESH
GROUPS, PARTS, XS, ZS, YS = 32, 16, 4, 8, 8
BLOCK = (LENGTH + 1) * ROWS
DEPTH = 128


def plan():
    copies = {}
    for d in (1, -1):
        for s in range(4):
            copies["kz", d, 0, s] = (("z", d), 128 if s < 3 else 64, [("kz", d, 0, s - 1)] if s else [])
        for q in range(-3, 5):
            need = [("kz", 1, 0, 3), ("kz", -1, 0, 3)] if q == 4 else [] if q == 0 else [("kz", -1 if q > 0 else 1, 0, abs(q) - 1)]
            copies["kx", d, q, 0] = (("x", d), 128, need)
            copies["kx", d, q, 1] = (("x", d), 64, [("kx", d, q, 0)])
        for s in range(2):
            copies["rx", d, 0, s] = (("x", d), 64 if s == 0 else 32, [("rx", d, 0, 0)] if s else [])
        for q in (0, -1, 1, 2):
            first = [("rx", 1, 0, 1), ("rx", -1, 0, 1)] if q == 2 else [] if q == 0 else [("rx", -q, 0, 0)]
            for s in range(4):
                copies["rz", d, q, s] = (("z", d), 64 if s < 3 else 32, [("rz", d, q, s - 1)] if s else first)
        for s in range(4):
            for half in range(2):
                if s == 3 and (half == 0) != (d == 1):
                    continue
                copies["ty", d, half, s] = (("y", d), 136, [("ty", d, half, s - 1)] if s else ["tokens"])
                copies["tc", d, half, s] = (("c", 0), 136, [("ty", d, half, s)])
    for half in range(2):
        copies["tc", 0, half, 0] = (("c", 0), 136, ["tokens"])
    return copies


def schedule(copies):
    rate = {"x": 46.0, "z": 46.0, "y": 46.0, "c": 200.0}
    free = {}
    for axis, busy in (("x", 7.0), ("z", 13.0), ("y", 0.0)):
        for d in (1, -1):
            free[axis, d] = busy
    free["c", 0] = 0.0
    lands, done, issued, steps = {"tokens": 16.0}, set(), set(), []

    def issue(now):
        for name, ((axis, d), size, need) in copies.items():
            if name not in issued and all(n in done for n in need):
                issued.add(name)
                start = max(now, free[axis, d])
                free[axis, d] = start + size * 1.024 / rate[axis]
                lands[name] = free[axis, d] + 1.5
                steps.append(("send", name))

    now = 1.0
    issue(now)
    while len(done) < len(copies) + 1:
        name = min((n for n in lands if n not in done), key=lambda n: lands[n])
        now = max(now, lands[name])
        done.add(name)
        steps.append(("arrive", name))
        issue(now)
    return steps


def gather_kernel(
    source_ref, row_ref, suffix_ref, shift_ref, wr_ref, wk_ref, wv_ref, blend_ref, down_ref,
    r_out, k_out, v_out, low_out, token_out,
    outbox, inbox, rows_f, tok, w, mixed, mixed_low, acc, low_acc,
    own_sem, swap_send, swap_recv, send_sem, recv_sem,
):
    me, part = lax.axis_index("req"), lax.axis_index("head")
    z, x = me // XS, me % XS
    yy, core = part // 2, part % 2

    def group_at(dz, dx):
        return ((z + dz + ZS) % ZS) * XS + (x + dx + XS) % XS

    def part_at(dy):
        return ((yy + dy + YS) % YS) * 2 + core

    partner = part + 1 - 2 * core

    own = []
    for q, ref in enumerate((wr_ref, wk_ref, wv_ref)):
        own.append(pltpu.make_async_copy(ref, w.at[q, pl.ds(pl.multiple_of(me * DEPTH, DEPTH), DEPTH)], own_sem.at[q]))
    for c in own:
        c.start()

    barrier = pltpu.get_barrier_semaphore()

    def greet(i, carry):
        pl.semaphore_signal(barrier, inc=1, device_id={"req": (me + i) % GROUPS}, device_id_type=MESH)
        return carry

    lax.fori_loop(1, GROUPS, greet, 0)
    for other in (part_at(1), part_at(-1), partner):
        pl.semaphore_signal(barrier, inc=1, device_id={"head": other}, device_id_type=MESH)

    def pack(i, carry):
        outbox[i] = suffix_ref[source_ref[i]]
        return carry

    lax.fori_loop(0, 2 * GROUPS, pack, 0, unroll=4)
    pl.semaphore_wait(barrier, GROUPS + 2)

    def swap(i):
        to = (me + i) % GROUPS
        return pltpu.make_async_remote_copy(
            src_ref=outbox.at[pl.ds(2 * to, 2)], dst_ref=inbox.at[pl.ds(2 * me, 2)],
            send_sem=swap_send.at[i], recv_sem=swap_recv.at[i], device_id={"req": to}, device_id_type=MESH,
        )

    def swap_in(i):
        source = inbox.at[pl.ds(2 * ((me - i + GROUPS) % GROUPS), 2)]
        return pltpu.make_async_remote_copy(
            src_ref=source, dst_ref=source, send_sem=swap_send.at[i], recv_sem=swap_recv.at[i],
            device_id={"req": (me + i) % GROUPS}, device_id_type=MESH,
        )

    def swap_start(i, carry):
        swap(i).start()
        return carry

    lax.fori_loop(1, GROUPS, swap_start, 0)
    for i in range(2):
        inbox[2 * me + i] = outbox[2 * me + i]
    for c in own:
        c.wait()

    def weight_rows(group, half):
        at = pl.multiple_of(group * DEPTH, DEPTH)
        if half is None:
            return pl.ds(at, DEPTH)
        return pl.ds(pl.multiple_of(at + half * 64, 64), 64)

    def place(name, arrival):
        kind, d, q, s = name
        back = d if arrival else 0
        half = 0 if d == 1 else 1
        if kind == "kz":
            return w.at[1:3, weight_rows(group_at(-d * s - back, 0), half if s == 3 else None)], {"req": group_at(d, 0)}
        if kind == "kx":
            return w.at[1:3, weight_rows(group_at(q, -d * s - back), half if s else None)], {"req": group_at(0, d)}
        if kind == "rx":
            return w.at[0, weight_rows(group_at(0, -d * s - back), half if s else None)], {"req": group_at(0, d)}
        if kind == "rz":
            return w.at[0, weight_rows(group_at(-d * s - back, q), half if s == 3 else None)], {"req": group_at(d, 0)}
        piece = pl.ds(q * (BLOCK // 2), BLOCK // 2)
        if kind == "ty":
            return tok.at[part_at(-d * s - back), piece], {"head": part_at(d)}
        source = part_at(-d * (s + 1)) if d else part
        if arrival:
            source = source + 1 - 2 * core
        return tok.at[source, piece], {"head": partner}

    copies = plan()
    number = {name: i for i, name in enumerate(copies)}

    def copy(name, arrival):
        ref, device = place(name, arrival)
        i = number[name]
        return pltpu.make_async_remote_copy(
            src_ref=ref, dst_ref=ref, send_sem=send_sem.at[i], recv_sem=recv_sem.at[i], device_id=device, device_id_type=MESH
        )

    def unpack():
        def wait(i, carry):
            swap_in(i).wait_recv()
            return carry

        lax.fori_loop(1, GROUPS, wait, 0)

        def row(n, carry):
            value = inbox[row_ref[n]].astype(F32)
            for e in range(2):
                rows_f[e, pl.ds(n, LENGTH, stride=ROWS), :] = value[:, e * 128 : (e + 1) * 128]
            return carry

        lax.fori_loop(0, ROWS, row, 0, unroll=4)
        tok[part, 0:ROWS] = shift_ref[...]
        tok[part, ROWS:BLOCK] = take(rows_f, slice(None)).astype(BF16)

    low_acc[...] = jnp.zeros_like(low_acc)

    def mix(source):
        columns = pl.ds(pl.multiple_of(source * WIDTH, WIDTH), WIDTH)
        blends = [blend_ref[q : q + 1, columns] for q in range(4)]

        def rows(i, carry):
            at = pl.ds(pl.multiple_of(i * 64, 64), 64)
            before = tok[source, at].astype(F32)
            now = tok[source, pl.ds(pl.multiple_of(i * 64 + ROWS, 32), 64)].astype(F32)
            change = before - now
            for q in range(3):
                mixed[q, at, columns] = (now + change * blends[q]).astype(BF16)
            mixed_low[at] = (now + change * blends[3]).astype(BF16)
            return carry

        lax.fori_loop(0, TOKENS // 64, rows, 0)
        low_acc[...] += mm(mixed_low[...], down_ref[columns])

    def project(q, out):
        acc[...] = jnp.zeros_like(acc)

        def rows(i, carry):
            at = pl.ds(pl.multiple_of(i * 512, 512), 512)
            acc[...] += mm(mixed[q, :, at], w[q, at])
            return carry

        lax.fori_loop(0, PARTS // 2, rows, 0)
        out[...] = acc[...].astype(BF16)

    arrived, pending = set(), []
    for verb, name in schedule(copies):
        if verb == "send":
            copy(name, False).start()
            continue
        if pending:
            mix(pending.pop(0))
        if name == "tokens":
            unpack()
            pending.append(part)
        else:
            copy(name, True).wait_recv()
        arrived.add(name)
        if name != "tokens" and name[0] in ("ty", "tc"):
            kind, d, half, s = name
            if kind == "tc" and d == 0:
                ready = {("tc", 0, 0, 0), ("tc", 0, 1, 0)} <= arrived
            elif s == 3:
                ready = {(kind, 1, 0, 3), (kind, -1, 1, 3)} <= arrived
            else:
                ready = {(kind, d, 0, s), (kind, d, 1, s)} <= arrived
            if ready:
                source = part if d == 0 else part_at(-d * (s + 1))
                pending.append(source if kind == "ty" else source + 1 - 2 * core)
    for source in pending:
        mix(source)
    low_out[...] = jnp.tanh(low_acc[...]).astype(BF16)
    token_out[...] = tok[part, ROWS:BLOCK]
    project(0, r_out)
    project(1, k_out)
    project(2, v_out)

    def drain(i, carry):
        swap(i).wait_send()
        return carry

    lax.fori_loop(1, GROUPS, drain, 0)
    for name in copies:
        copy(name, False).wait_send()


def gather(source, row, suffix, shift, wr, wk, wv, blend, down):
    vm, sm, hbm = (pl.BlockSpec(memory_space=s) for s in (pltpu.VMEM, pltpu.SMEM, pl.ANY))
    tokens = jax.ShapeDtypeStruct((TOKENS, WIDTH), BF16)
    count = len(plan())
    return pl.pallas_call(
        gather_kernel,
        out_shape=(tokens, tokens, tokens, jax.ShapeDtypeStruct((TOKENS, DEPTH), BF16), tokens),
        in_specs=[sm, sm, vm, vm, hbm, hbm, hbm, vm, vm],
        out_specs=(vm,) * 5,
        scratch_shapes=[
            pltpu.VMEM((2 * GROUPS, LENGTH, WIDTH), BF16),
            pltpu.VMEM((2 * GROUPS, LENGTH, WIDTH), BF16),
            pltpu.VMEM((2, TOKENS, 128), F32),
            pltpu.VMEM((PARTS, BLOCK, WIDTH), BF16),
            pltpu.VMEM((3, GROUPS * DEPTH, WIDTH), BF16),
            pltpu.VMEM((3, TOKENS, PARTS * WIDTH), BF16),
            pltpu.VMEM((TOKENS, WIDTH), BF16),
            pltpu.VMEM((TOKENS, WIDTH), F32),
            pltpu.VMEM((TOKENS, DEPTH), F32),
            pltpu.SemaphoreType.DMA((3,)),
            pltpu.SemaphoreType.DMA((GROUPS,)),
            pltpu.SemaphoreType.DMA((GROUPS,)),
            pltpu.SemaphoreType.DMA((count,)),
            pltpu.SemaphoreType.DMA((count,)),
        ],
        compiler_params=pltpu.CompilerParams(collective_id=0, has_side_effects=True, vmem_limit_bytes=60000 * 1024),
        name="gather",
    )(source, row, suffix, shift, wr, wk, wv, blend, down)

def on_device(
    suffix_embeddings,
    suffix_extents,
    memory_line_pointer,
    previous_token_store,
    stored_memories,
    blend_fractions,
    acceptor_linear,
    address_linear,
    payload_linear,
    fading_baseline,
    fading_bottleneck_down,
    fading_bottleneck_up,
    self_reward,
    team_normalizer_gain,
):
    group = lax.axis_index("req")
    owners = (memory_line_pointer // ROWS).reshape(GROUPS, ROWS)
    earlier = jnp.arange(ROWS)[:, None] > jnp.arange(ROWS)[None, :]
    rank = jnp.sum(((owners[:, :, None] == owners[:, None, :]) & earlier[None]).astype(jnp.int32), axis=2)
    inbox_slot = (jnp.arange(GROUPS, dtype=jnp.int32)[:, None] * 2 + rank).reshape(-1)
    outbox_slot = lax.dynamic_index_in_dim(owners * 2 + rank, group, 0, keepdims=False)
    here = memory_line_pointer[None, :] == (group * ROWS + jnp.arange(ROWS, dtype=jnp.int32))[:, None]
    row_slot = jnp.sum(jnp.where(here, inbox_slot[None, :], 0), axis=1)
    row_extent = jnp.sum(jnp.where(here, suffix_extents[None, :], 0), axis=1)
    wanted = outbox_slot[None, :] == jnp.arange(2 * GROUPS, dtype=jnp.int32)[:, None]
    source = jnp.sum(jnp.where(wanted, jnp.arange(ROWS, dtype=jnp.int32)[None, :], 0), axis=1)
    r, k, v, low, tokens = gather(
        source, row_slot, suffix_embeddings, previous_token_store,
        acceptor_linear, address_linear, payload_linear, blend_fractions, fading_bottleneck_down,
    )
    state = stored_memories.reshape(ROWS, TEAMS, 32, 128).transpose(0, 2, 1, 3).reshape(ROWS, 128, 128)
    extents = jnp.broadcast_to(row_extent[:, None], (ROWS, 128))
    outbox, new_state, new_shift = recurrence(
        row_slot, r, k, v, low, fading_bottleneck_up, fading_baseline, self_reward, team_normalizer_gain, extents, state, tokens
    )
    inbox = lax.all_to_all(outbox, "req", split_axis=0, concat_axis=0, tiled=True)
    mixed_out = inbox[outbox_slot]
    new_state = new_state.reshape(ROWS, 32, TEAMS, 128).transpose(0, 2, 1, 3).reshape(ROWS, TEAMS, 4096)
    return (mixed_out, new_state, new_shift)


def solution(mesh):
    placed = (
        P("req", None, "head"),
        P(),
        P(),
        P("req", "head"),
        P("req", "head", None),
        P(),
        P("req", "head"),
        P("req", "head"),
        P("req", "head"),
        P("head"),
        P(),
        P(None, "head"),
        P("head"),
        P("head"),
    )
    return jax.shard_map(
        on_device,
        mesh=mesh,
        in_specs=placed,
        out_specs=(P("req", None, "head"), P("req", "head", None), P("req", "head")),
        check_vma=False,
    )
```
